128 devices in a mesh: seg: 8 (over z, core), sec: 16 (over y, x).
Axes of the slice: x: 4, y: 4, z: 4, core: 2. Of those that a mesh axis runs over, the one named last changes fastest.
Arguments:
- wave_block: bfloat16 [8, 4096, 128, 128], P('seg', 'sec'), may hold values from -6 to 6
- left_envs: bfloat16 [8, 128, 128, 24, 128], P('seg', 'sec'), may hold values from -0.109375 to 0.109375
- next_vectors: bfloat16 [8, 128, 128, 1024], P('seg', 'sec'), may hold values from -6 to 6
- site_weights: float32 [8, 24, 1024], P('seg'), may hold values from 0.5 to 2
- kept_counts: int32 [128], replicated, may hold values from 32 to 128
- slots_before: int32 [128], replicated, may hold values from 0 to 127, as said below
- slots_after: int32 [128], replicated, may hold values from 0 to 127, as said below
Outputs:
- mixed_out: bfloat16 [8, 128, 128, 1024], P('seg', 'sec')
The draws below stay inside these ranges and needn't reach their ends.
Inputs may be any that keep to these rules, and one draw needn't show every extreme that they name: `slots_before`: A permutation of the sectors; device p of sec holds before-slots p * 8 to (p + 1) * 8 - 1. `slots_after`: A permutation of the sectors; device p of sec holds after-slots p * 8 to (p + 1) * 8 - 1. Of the sectors in one device's before-slots, at most 1 lie in any one device's after-slots, and exactly 1 for some pair of devices.
All inputs are finite; a program needn't handle non-finite values.
Results may differ from the reference program's by a relative error of at most 0.0058.
Values may be sent and summed in bfloat16 or wider, within the bound.
No kernel may reach another device: no remote copies, remote signals or barrier semaphores. Data moves between devices by JAX's collectives and lax.ppermute only.
A program may use at most 192 MiB of HBM per device.

```python
import math
import jax
import jax.numpy as jnp
from jax import lax

M = 128
KW = 24
SD = 8
CAP = 1
COLS = 1024
NSECT = 128
ROWS = 4096
SEGS = 8
N_SEC = 16


def sector_maps(key):
    before = jax.random.permutation(jax.random.fold_in(key, 11), NSECT).astype(jnp.int32)
    offsets = jax.random.permutation(jax.random.fold_in(key, 12), N_SEC)[:SD // CAP].astype(jnp.int32)
    shifts = jnp.repeat(offsets, CAP)
    devices = jnp.arange(N_SEC, dtype=jnp.int32)
    places = jnp.arange(SD, dtype=jnp.int32)
    source_dev = (devices[:, None] - shifts[None, :]) % N_SEC
    sectors = jnp.take(before, source_dev * SD + places[None, :])
    scores = jax.random.randint(jax.random.fold_in(key, 13), (N_SEC, SD), 0, 1048576) * SD + places[None, :]
    shuffle = jnp.argsort(scores, axis=1, stable=True)
    after = jnp.take_along_axis(sectors, shuffle, axis=1)
    return (before, after.reshape(NSECT).astype(jnp.int32))


def draw_slots_before(key, part):
    return sector_maps(key)[0]


def draw_slots_after(key, part):
    return sector_maps(key)[1]


def plant(result, own_key, least, top_value):
    dims = result.shape
    spot = [jax.random.randint(jax.random.fold_in(own_key, axis), (), 0, dims[axis]) for axis in range(len(dims))]
    result = result.at[tuple(spot)].set(least)
    longest = dims.index(max(dims))
    spot[longest] = (spot[longest] + 1) % dims[longest]
    return result.at[tuple(spot)].set(top_value)


def block_levels(own_key, extent, pieces, smallest, high):
    loudness = 1.0
    for axis_at, parts in pieces:
        heights = jax.random.uniform(jax.random.fold_in(jax.random.fold_in(own_key, 6), axis_at), (parts,), jnp.float32, smallest / len(pieces), high / len(pieces))
        loudness = loudness * jnp.repeat(jnp.exp(heights), extent[axis_at] // parts).reshape((-1,) + (1,) * (len(extent) - 1 - axis_at))
    return loudness


def bell_draw(own_key, extent, deviation, bound, shards=(), held_as=jnp.bfloat16):
    array = deviation * jax.random.normal(own_key, extent, jnp.float32)
    if shards:
        array = array * block_levels(own_key, extent, shards, -0.22, 0.18)
    return jnp.clip(array, -bound, bound).astype(held_as)


def setup_inputs(seed: int = 0) -> dict:
    keys = jax.random.split(jax.random.key(seed), 8)
    wave_block = bell_draw(keys[0], (SEGS, ROWS, NSECT, M), 1.0, 6.0, ((0, 8), (1, 16)))
    left_envs = bell_draw(keys[1], (SEGS, NSECT, M, KW, M), (KW * M) ** -0.5, 0.109375, ((0, 8), (1, 16)))
    next_vectors = bell_draw(keys[2], (SEGS, NSECT, M, COLS), 1.0, 6.0, ((0, 8), (1, 16)))
    site_weights = jnp.clip(jnp.exp(math.log(2.0) - 1.3862944 * jax.random.uniform(keys[3], (SEGS, KW, COLS), jnp.float32) ** block_levels(keys[3], (SEGS, KW, COLS), ((0, 8),), -0.2, 0.2)), 0.5, 2.0)
    kept_counts = plant(jax.random.randint(keys[4], (NSECT,), M // 4, M + 1), jax.random.fold_in(keys[4], 1), M // 4, M).astype(jnp.int32)
    slots_before = draw_slots_before(jax.random.fold_in(keys[7], 71), 0)
    slots_after = draw_slots_after(jax.random.fold_in(keys[7], 71), 0)
    return {"wave_block": wave_block, "left_envs": left_envs, "next_vectors": next_vectors, "site_weights": site_weights, "kept_counts": kept_counts, "slots_before": slots_before, "slots_after": slots_after}


def inverse_of(slots):
    length_of = slots.shape[0]
    indices = jnp.arange(length_of, dtype=jnp.int32)
    return jnp.sum(jnp.where(slots[:, None] == indices[None, :], indices[:, None], 0), axis=0).astype(jnp.int32)

def reference(wave_block, left_envs, next_vectors, site_weights, kept_counts, slots_before, slots_after):
    identity = jnp.eye(M, dtype=jnp.float32)
    channel_zero = (jnp.arange(KW) == 0).astype(jnp.float32)
    boundary = identity[:, None, :] * channel_zero[None, :, None]
    boundary = jnp.broadcast_to(boundary[None], (NSECT, M, KW, M))
    incoming = jnp.concatenate([boundary[None], left_envs[:-1].astype(jnp.float32)], axis=0)
    inv_before = inverse_of(slots_before)
    moved = jnp.take(inv_before, slots_after)
    kept_slots = jnp.take(kept_counts, slots_before)
    keep_mask = (jnp.arange(M)[None, :] < kept_slots[:, None]).astype(jnp.float32)

    def segment(inputs):
        wave, env_in, vectors, weights = inputs
        wide = wave.astype(jnp.float32)
        gram_sum = jnp.einsum('rsa,rsb->sab', wide, wide, precision=lax.Precision.HIGHEST)
        gram_sum = gram_sum / ROWS + 0.1 * identity
        gram_slots = jnp.take(gram_sum, slots_before, axis=0)
        factor = jnp.linalg.cholesky(gram_slots)
        inverse = lax.linalg.triangular_solve(factor, jnp.broadcast_to(identity, gram_slots.shape), left_side=True, lower=True)
        inverse = inverse * keep_mask[:, :, None]
        truncated = jnp.einsum('sab,sbwc,sdc->sawd', inverse, env_in, inverse, precision=lax.Precision.HIGHEST).astype(jnp.bfloat16)
        arranged = jnp.take(truncated, moved, axis=0)

        def sector(pair):
            blocks, block_vec = pair
            scaled = (block_vec.astype(jnp.float32)[None] * weights[:, None, :]).astype(jnp.bfloat16)
            return jnp.einsum('awd,wdc->ac', blocks.astype(jnp.float32), scaled.astype(jnp.float32), precision=lax.Precision.HIGHEST).astype(jnp.bfloat16)
        return lax.map(sector, (arranged, vectors))
    return lax.map(segment, (wave_block, incoming, next_vectors, site_weights))
```

```python
import functools

import jax
import jax.numpy as jnp
from jax import lax
from jax.experimental import pallas as pl
from jax.experimental.pallas import tpu as pltpu
from jax.sharding import PartitionSpec as P

F32 = jnp.float32
BF16 = jnp.bfloat16


def whole(shape):
    return pl.BlockSpec(shape, lambda *_: (0,) * len(shape))


def passed_along(value, axis, steps):
    count = lax.axis_size(axis)
    first, last = (max(0, -steps), min(count, count - steps))
    return lax.ppermute(value, axis, [(source, source + steps) for source in range(first, last)])


def iota2(shape, axis):
    return lax.broadcasted_iota(jnp.int32, shape, axis)


def prologue_kernel(
    where_ref, before_ref, after_ref, kept_ref, vec_ref,
    packed_ref, place_ref, table_ref, inv_ref, sems,
):
    width = vec_ref.shape[0]
    total = before_ref.shape[0]
    base = where_ref[0] * width

    def invert(i, carry):
        place_ref[before_ref[i]] = i
        inv_ref[after_ref[i]] = i
        return carry

    lax.fori_loop(0, total, invert, 0)
    copies = []
    for j in range(width):
        to = place_ref[after_ref[base + j]] // width
        copy = pltpu.make_async_copy(vec_ref.at[j], packed_ref.at[to], sems.at[j])
        copy.start()
        copies.append(copy)
        sector = before_ref[base + j]
        table_ref[j] = inv_ref[sector] // width
        table_ref[width + j] = to
        table_ref[2 * width + j] = kept_ref[sector]
        table_ref[3 * width + j] = where_ref[1]
    for copy in copies:
        copy.wait()


def prologue(where, before, after, kept, vectors, devices):
    width, size, cols = vectors.shape
    total = before.shape[0]
    smem = pl.BlockSpec(memory_space=pltpu.SMEM)
    hbm = pl.BlockSpec(memory_space=pl.ANY)
    return pl.pallas_call(
        prologue_kernel,
        out_shape=(
            jax.ShapeDtypeStruct((devices, size, cols), vectors.dtype),
            jax.ShapeDtypeStruct((total,), jnp.int32),
            jax.ShapeDtypeStruct((4 * width,), jnp.int32),
        ),
        in_specs=[smem, smem, smem, smem, hbm],
        out_specs=(hbm, smem, smem),
        scratch_shapes=[pltpu.SMEM((total,), jnp.int32), pltpu.SemaphoreType.DMA((width,))],
        name="prologue",
    )(where, before, after, kept, vectors)


def gram_kernel(place_ref, x_ref, o_ref, diag_ref, *, width):
    step = pl.program_id(0)
    count, size = x_ref.shape[1:]
    half = size // 2
    turned = jnp.swapaxes(x_ref[...], 0, 1)
    row, lane = iota2((half, size), 0), iota2((half, size), 1)
    from_top = (lane >= half) & (row >= lane - half)
    on_diag = iota2((size, size), 0) == iota2((size, size), 1)
    for k in range(count):
        block = turned[k]
        full = lax.dot_general(
            block, block, (((0,), (0,)), ((), ())), preferred_element_type=F32
        )
        at = place_ref[step * count + k]
        packed = jnp.where(from_top, pltpu.roll(full[:half], half, 1), full[half:])
        start = pl.multiple_of((at % width) * half, half)
        o_ref[at // width, pl.ds(start, half), :] = packed.astype(BF16)
        diag_ref[pl.ds(at, 1), :] = jnp.sum(jnp.where(on_diag, full, 0.0), axis=0, keepdims=True)

    @pl.when(step == pl.num_programs(0) - 1)
    def _():
        for t in range(o_ref.shape[0]):
            exact = diag_ref[t * width : (t + 1) * width, :]
            high = exact.astype(BF16).astype(F32)
            both = jnp.concatenate([high, exact - high], axis=0)
            o_ref[t, width * half :, :] = both.astype(BF16)


def partial_grams(place, rows, width, count=32):
    length, sectors, size = rows.shape
    devices = sectors // width
    shape = (devices, width * (size // 2) + 2 * width, size)
    return pl.pallas_call(
        functools.partial(gram_kernel, width=width),
        out_shape=jax.ShapeDtypeStruct(shape, BF16),
        grid_spec=pltpu.PrefetchScalarGridSpec(
            num_scalar_prefetch=1,
            grid=(sectors // count,),
            in_specs=[pl.BlockSpec((length, count, size), lambda i, _: (0, i, 0))],
            out_specs=whole(shape),
            scratch_shapes=[pltpu.VMEM((sectors, size), F32)],
        ),
        name="gram",
    )(place, rows)


def split3(value):
    high = value.astype(BF16)
    rest = value - high.astype(F32)
    mid = rest.astype(BF16)
    low = (rest - mid.astype(F32)).astype(BF16)
    return high, mid, low


def factor_kernel(table_ref, g_ref, right_ref, left_ref, state_ref, *, total_rows):
    width, size, _ = state_ref.shape
    half = size // 2
    devices = g_ref.shape[0]
    summed = g_ref[0].astype(F32)
    for t in range(1, devices):
        summed = summed + g_ref[t].astype(F32)
    scale = 1.0 / total_rows
    diag = (summed[width * half : width * half + width] + summed[width * half + width :]) * scale
    packed = (summed[: width * half] * scale).reshape(width, half, size)
    lane = iota2((half, size), 1)
    row2, lane2 = iota2((size, size), 0), iota2((size, size), 1)
    for m in range(width):
        p = packed[m]
        turned = jnp.concatenate([p, p], axis=0).T
        top = jnp.where(lane >= half, turned[:half], pltpu.roll(turned[half:], half, 1))
        upper = jnp.concatenate([top, p], axis=0)
        both = jnp.where(lane2 > row2, upper, upper.T)
        state_ref[m] = jnp.where(lane2 == row2, diag[m : m + 1] + 0.1, both)

    lane8, sub8 = iota2((8, size), 1), iota2((8, size), 0)
    for r0 in range(0, size, 8):
        panel = state_ref[:, r0 : r0 + 8, :]
        for k in range(8):
            c = r0 + k
            col = panel[:, :, c : c + 1]
            pivot = panel[:, k : k + 1, c : c + 1]
            rk = lax.rsqrt(pivot)
            rk = rk * (1.5 - 0.5 * pivot * rk * rk)
            lead = jnp.where(lane8[:1] == c, rk, panel[:, k : k + 1, :] * rk)
            kept = jnp.where(lane8 == c, 0.0, panel) - (col * rk) * lead
            panel = jnp.where(sub8 > k, kept, jnp.where(sub8 == k, lead, panel))
        rest = r0 + 8
        panel = jnp.where((lane8 < rest) & (lane8 > r0 + sub8), 0.0, panel)
        state_ref[:, r0:rest, :] = panel
        if rest < size:
            h, m_, l = split3(panel)
            one = jnp.concatenate([h, h, h, m_, m_, l], axis=1)
            two = jnp.concatenate([h, m_, l, h, m_, h], axis=1)
            inside = (lane2[rest:] >= r0) & (lane2[rest:] < rest)
            for m in range(width):
                update = lax.dot_general(
                    one[m], two[m], (((0,), (0,)), ((), ())), preferred_element_type=F32
                )
                old = jnp.where(inside, 0.0, state_ref[m, rest:, :])
                state_ref[m, rest:, :] = old - update[rest:]

    for m in range(width):
        inverse = jnp.where(
            (lane2 <= row2) & (row2 < table_ref[2 * width + m]), state_ref[m], 0.0
        )
        high, low, _ = split3(inverse)
        left_ref[m] = jnp.concatenate([high, low, high], axis=1)
        high, low, _ = split3(inverse.T)
        right_ref[m] = jnp.concatenate([high, low], axis=1)


def inverse_factors(table, grams, width, total_rows):
    size = grams.shape[2]
    shapes = ((width, size, 2 * size), (width, size, 3 * size))
    return pl.pallas_call(
        functools.partial(factor_kernel, total_rows=total_rows),
        out_shape=tuple(jax.ShapeDtypeStruct(s, BF16) for s in shapes),
        grid_spec=pltpu.PrefetchScalarGridSpec(
            num_scalar_prefetch=1,
            grid=(1,),
            in_specs=[whole(grams.shape)],
            out_specs=tuple(whole(s) for s in shapes),
            scratch_shapes=[pltpu.VMEM((width, size, size), F32)],
        ),
        name="factor",
    )(table, grams)


def matvec_kernel(table_ref, v_ref, e_ref, w_ref, right_ref, left_ref, o_ref, *, width, group):
    channels, size = e_ref.shape[2:]
    v = v_ref[0]
    y = jnp.dot(right_ref[0], jnp.concatenate([v, v], axis=0), preferred_element_type=F32)
    env = jnp.swapaxes(e_ref[0], 0, 1)
    eye = (iota2((size, size), 0) == iota2((size, size), 1)).astype(BF16)
    first = table_ref[3 * width] == 0
    total = None
    for w in range(0, channels, group):
        blocks, scaled = [], []
        for u in range(w, w + group):
            block = env[u]
            blocks.append(jnp.where(first, eye if u == 0 else jnp.zeros_like(eye), block))
            scaled.append((y * w_ref[u : u + 1, :]).astype(BF16))
        part = jnp.dot(
            jnp.concatenate(blocks, axis=1),
            jnp.concatenate(scaled, axis=0),
            preferred_element_type=F32,
        )
        total = part if total is None else total + part
    high = total.astype(BF16)
    low = (total - high.astype(F32)).astype(BF16)
    o_ref[0] = jnp.dot(
        left_ref[0], jnp.concatenate([high, high, low], axis=0), preferred_element_type=F32
    ).astype(BF16)


def matvec(table, arrived, env, weights, right, left, group=4):
    width, size, channels, _ = env.shape
    devices, _, cols = arrived.shape
    at = pl.BlockSpec((1, size, cols), lambda i, t: (t[i], 0, 0))
    return pl.pallas_call(
        functools.partial(matvec_kernel, width=width, group=group),
        out_shape=jax.ShapeDtypeStruct((devices, size, cols), BF16),
        grid_spec=pltpu.PrefetchScalarGridSpec(
            num_scalar_prefetch=1,
            grid=(width,),
            in_specs=[
                at,
                pl.BlockSpec((1, size, channels, size), lambda i, t: (i, 0, 0, 0)),
                whole(weights.shape),
                pl.BlockSpec((1, size, 2 * size), lambda i, t: (i, 0, 0)),
                pl.BlockSpec((1, size, 3 * size), lambda i, t: (i, 0, 0)),
            ],
            out_specs=at,
        ),
        name="matvec",
    )(table, arrived, env, weights, right, left)


def gather_kernel(table_ref, x_ref, o_ref):
    o_ref[...] = x_ref[...]


def gathered(table, returned, width):
    devices, size, cols = returned.shape
    return pl.pallas_call(
        gather_kernel,
        out_shape=jax.ShapeDtypeStruct((width, size, cols), BF16),
        grid_spec=pltpu.PrefetchScalarGridSpec(
            num_scalar_prefetch=1,
            grid=(width,),
            in_specs=[pl.BlockSpec((1, size, cols), lambda j, t: (t[width + j], 0, 0))],
            out_specs=pl.BlockSpec((1, size, cols), lambda j, t: (j, 0, 0)),
        ),
        name="gather",
    )(table, returned)


def exchange(value):
    return lax.all_to_all(value, "sec", split_axis=0, concat_axis=0, tiled=True)


def on_device(
    wave_block, left_envs, next_vectors, site_weights, kept_counts, slots_before, slots_after
):
    devices = lax.axis_size("sec")
    width = left_envs.shape[1]
    previous = passed_along(left_envs[0], "seg", 1)
    where = jnp.stack([lax.axis_index("sec"), lax.axis_index("seg")]).astype(jnp.int32)
    packed, place, table = prologue(
        where, slots_before, slots_after, kept_counts, next_vectors[0], devices
    )
    arrived = exchange(packed)
    grams = exchange(partial_grams(place, wave_block[0], width))
    right, left = inverse_factors(table, grams, width, wave_block.shape[1] * devices)
    result = matvec(table, arrived, previous, site_weights[0], right, left)
    return gathered(table, exchange(result), width)[None]


def solution(mesh):
    placed = (
        P("seg", "sec", None, None),
        P("seg", "sec", None, None, None),
        P("seg", "sec", None, None),
        P("seg", None, None),
        P(),
        P(),
        P(),
    )
    return jax.shard_map(
        on_device,
        mesh=mesh,
        in_specs=placed,
        out_specs=P("seg", "sec", None, None),
        check_vma=False,
    )
```

```python
import functools

import jax
import jax.numpy as jnp
from jax import lax
from jax.experimental import pallas as pl
from jax.experimental.pallas import tpu as pltpu
from jax.sharding import PartitionSpec as P


F32 = jnp.float32
BF16 = jnp.bfloat16


def whole(shape):
    return pl.BlockSpec(shape, lambda *_: (0,) * len(shape))


def passed_along(value, axis, steps):
    count = lax.axis_size(axis)
    first, last = (max(0, -steps), min(count, count - steps))
    return lax.ppermute(value, axis, [(source, source + steps) for source in range(first, last)])


def iota2(shape, axis):
    return lax.broadcasted_iota(jnp.int32, shape, axis)


def prologue_kernel(
    where_ref, before_ref, after_ref, kept_ref, vec_ref, place_ref, table_ref, *rest
):
    packed_refs, (inv_ref, sems) = rest[:-2], rest[-2:]
    width = vec_ref.shape[0]
    total = before_ref.shape[0]
    base = where_ref[0] * width
    cols = packed_refs[0].shape[2]

    def invert(i, carry):
        place_ref[before_ref[i]] = i
        inv_ref[after_ref[i]] = i
        return carry

    lax.fori_loop(0, total, invert, 0)
    for j in range(width):
        table_ref[width + j] = place_ref[after_ref[base + j]] // width
    copies = [
        pltpu.make_async_copy(
            vec_ref.at[j, :, pl.ds(h * cols, cols)],
            packed.at[table_ref[width + j]],
            sems.at[h, j],
        )
        for h, packed in enumerate(packed_refs)
        for j in range(width)
    ]
    for copy in copies:
        copy.start()
    for j in range(width):
        sector = before_ref[base + j]
        table_ref[j] = inv_ref[sector] // width
        table_ref[2 * width + j] = kept_ref[sector]
        table_ref[3 * width + j] = where_ref[1]
    for copy in copies:
        copy.wait()


def prologue(where, before, after, kept, vectors, devices, parts):
    width, size, cols = vectors.shape
    total = before.shape[0]
    smem = pl.BlockSpec(memory_space=pltpu.SMEM)
    hbm = pl.BlockSpec(memory_space=pl.ANY)
    packed = jax.ShapeDtypeStruct((devices, size, cols // parts), vectors.dtype)
    place, table, *packs = pl.pallas_call(
        prologue_kernel,
        out_shape=(
            jax.ShapeDtypeStruct((total,), jnp.int32),
            jax.ShapeDtypeStruct((4 * width,), jnp.int32),
        )
        + (packed,) * parts,
        in_specs=[smem, smem, smem, smem, pl.BlockSpec(memory_space=pltpu.VMEM)],
        out_specs=(smem, smem) + (hbm,) * parts,
        scratch_shapes=[
            pltpu.SMEM((total,), jnp.int32),
            pltpu.SemaphoreType.DMA((parts, width)),
        ],
        name="prologue",
    )(where, before, after, kept, vectors)
    return place, table, packs


def gram_kernel(place_ref, x_ref, o_ref, diag_ref, *, width):
    step = pl.program_id(0)
    count, size = x_ref.shape[1:]
    half = size // 2
    turned = jnp.swapaxes(x_ref[...], 0, 1)
    row, lane = iota2((half, size), 0), iota2((half, size), 1)
    from_top = (lane >= half) & (row >= lane - half)
    on_diag = iota2((size, size), 0) == iota2((size, size), 1)
    for k in range(count):
        block = turned[k]
        full = lax.dot_general(
            block, block, (((0,), (0,)), ((), ())), preferred_element_type=F32
        )
        at = place_ref[step * count + k]
        packed = jnp.where(from_top, pltpu.roll(full[:half], half, 1), full[half:])
        start = pl.multiple_of((at % width) * half, half)
        o_ref[at // width, pl.ds(start, half), :] = packed.astype(BF16)
        diag_ref[pl.ds(at, 1), :] = jnp.sum(jnp.where(on_diag, full, 0.0), axis=0, keepdims=True)

    @pl.when(step == pl.num_programs(0) - 1)
    def _():
        for t in range(o_ref.shape[0]):
            exact = diag_ref[t * width : (t + 1) * width, :]
            high = exact.astype(BF16).astype(F32)
            both = jnp.concatenate([high, exact - high], axis=0)
            o_ref[t, width * half :, :] = both.astype(BF16)


def partial_grams(place, rows, width, count=32):
    length, sectors, size = rows.shape
    devices = sectors // width
    shape = (devices, width * (size // 2) + 2 * width, size)
    return pl.pallas_call(
        functools.partial(gram_kernel, width=width),
        out_shape=jax.ShapeDtypeStruct(shape, BF16),
        grid_spec=pltpu.PrefetchScalarGridSpec(
            num_scalar_prefetch=1,
            grid=(sectors // count,),
            in_specs=[pl.BlockSpec((length, count, size), lambda i, _: (0, i, 0))],
            out_specs=whole(shape),
            scratch_shapes=[pltpu.VMEM((sectors, size), F32)],
        ),
        name="gram",
    )(place, rows)


def split3(value):
    high = value.astype(BF16)
    rest = value - high.astype(F32)
    mid = rest.astype(BF16)
    low = (rest - mid.astype(F32)).astype(BF16)
    return high, mid, low


def factor_kernel(table_ref, g_ref, right_ref, left_ref, state_ref, *, total_rows):
    width, size, _ = state_ref.shape
    half = size // 2
    devices = g_ref.shape[0]
    summed = g_ref[0].astype(F32)
    for t in range(1, devices):
        summed = summed + g_ref[t].astype(F32)
    scale = 1.0 / total_rows
    diag = (summed[width * half : width * half + width] + summed[width * half + width :]) * scale
    packed = (summed[: width * half] * scale).reshape(width, half, size)
    lane = iota2((half, size), 1)
    row2, lane2 = iota2((size, size), 0), iota2((size, size), 1)
    for m in range(width):
        p = packed[m]
        turned = jnp.concatenate([p, p], axis=0).T
        top = jnp.where(lane >= half, turned[:half], pltpu.roll(turned[half:], half, 1))
        upper = jnp.concatenate([top, p], axis=0)
        both = jnp.where(lane2 > row2, upper, upper.T)
        state_ref[m] = jnp.where(lane2 == row2, diag[m : m + 1] + 0.1, both)

    lane8, sub8 = iota2((8, size), 1), iota2((8, size), 0)
    for r0 in range(0, size, 8):
        panel = state_ref[:, r0 : r0 + 8, :]
        for k in range(8):
            c = r0 + k
            col = panel[:, :, c : c + 1]
            pivot = panel[:, k : k + 1, c : c + 1]
            rk = lax.rsqrt(pivot)
            rk = rk * (1.5 - 0.5 * pivot * rk * rk)
            lead = jnp.where(lane8[:1] == c, rk, panel[:, k : k + 1, :] * rk)
            kept = jnp.where(lane8 == c, 0.0, panel) - (col * rk) * lead
            panel = jnp.where(sub8 > k, kept, jnp.where(sub8 == k, lead, panel))
        rest = r0 + 8
        panel = jnp.where((lane8 < rest) & (lane8 > r0 + sub8), 0.0, panel)
        state_ref[:, r0:rest, :] = panel
        if rest < size:
            h, m_, l = split3(panel)
            one = jnp.concatenate([h, h, h, m_, m_, l], axis=1)
            two = jnp.concatenate([h, m_, l, h, m_, h], axis=1)
            inside = (lane2[rest:] >= r0) & (lane2[rest:] < rest)
            for m in range(width):
                update = lax.dot_general(
                    one[m], two[m], (((0,), (0,)), ((), ())), preferred_element_type=F32
                )
                old = jnp.where(inside, 0.0, state_ref[m, rest:, :])
                state_ref[m, rest:, :] = old - update[rest:]

    for m in range(width):
        inverse = jnp.where(
            (lane2 <= row2) & (row2 < table_ref[2 * width + m]), state_ref[m], 0.0
        )
        high, low, _ = split3(inverse)
        left_ref[m] = jnp.concatenate([high, low, high], axis=1)
        high, low, _ = split3(inverse.T)
        right_ref[m] = jnp.concatenate([high, low], axis=1)


def inverse_factors(table, grams, width, total_rows):
    size = grams.shape[2]
    shapes = ((width, size, 2 * size), (width, size, 3 * size))
    return pl.pallas_call(
        functools.partial(factor_kernel, total_rows=total_rows),
        out_shape=tuple(jax.ShapeDtypeStruct(s, BF16) for s in shapes),
        grid_spec=pltpu.PrefetchScalarGridSpec(
            num_scalar_prefetch=1,
            grid=(1,),
            in_specs=[whole(grams.shape)],
            out_specs=tuple(whole(s) for s in shapes),
            scratch_shapes=[pltpu.VMEM((width, size, size), F32)],
        ),
        name="factor",
    )(table, grams)


def matvec_kernel(table_ref, v_ref, e_ref, w_ref, right_ref, left_ref, o_ref, *saved, width, group):
    channels, size = w_ref.shape[0], v_ref.shape[1]
    v = v_ref[0]
    y = jnp.dot(right_ref[0], jnp.concatenate([v, v], axis=0), preferred_element_type=F32)
    if saved:
        env = jnp.swapaxes(e_ref[0], 0, 1)
        eye = (iota2((size, size), 0) == iota2((size, size), 1)).astype(BF16)
        first = table_ref[3 * width] == 0
    total = None
    for w in range(0, channels, group):
        scaled = []
        for u in range(w, w + group):
            if saved:
                alone = eye if u == 0 else jnp.zeros_like(eye)
                saved[0][0, :, u * size : (u + 1) * size] = jnp.where(first, alone, env[u])
            scaled.append((y * w_ref[u : u + 1, :]).astype(BF16))
        here = saved[0] if saved else e_ref
        part = jnp.dot(
            here[0, :, w * size : (w + group) * size],
            jnp.concatenate(scaled, axis=0),
            preferred_element_type=F32,
        )
        total = part if total is None else total + part
    high = total.astype(BF16)
    low = (total - high.astype(F32)).astype(BF16)
    o_ref[0] = jnp.dot(
        left_ref[0], jnp.concatenate([high, high, low], axis=0), preferred_element_type=F32
    ).astype(BF16)


def matvec(table, arrived, env, weights, right, left, part, group=4):
    width, size, _ = right.shape
    channels = weights.shape[0]
    devices, _, cols = arrived.shape
    at = pl.BlockSpec((1, size, cols), lambda i, t: (t[i], 0, 0))
    wide = pl.BlockSpec((1, size, channels * size), lambda i, t: (i, 0, 0))
    out_shape = [jax.ShapeDtypeStruct((devices, size, cols), BF16)]
    out_specs = [at]
    if part == 0:
        out_shape.append(jax.ShapeDtypeStruct((width, size, channels * size), BF16))
        out_specs.append(wide)
    return pl.pallas_call(
        functools.partial(matvec_kernel, width=width, group=group),
        out_shape=out_shape,
        grid_spec=pltpu.PrefetchScalarGridSpec(
            num_scalar_prefetch=1,
            grid=(width,),
            in_specs=[
                at,
                pl.BlockSpec((1, size, channels, size), lambda i, t: (i, 0, 0, 0))
                if part == 0
                else wide,
                pl.BlockSpec((channels, cols), lambda i, t: (0, part)),
                pl.BlockSpec((1, size, 2 * size), lambda i, t: (i, 0, 0)),
                pl.BlockSpec((1, size, 3 * size), lambda i, t: (i, 0, 0)),
            ],
            out_specs=out_specs,
        ),
    )(table, arrived, env, weights, right, left)


def gather_kernel(table_ref, x_ref, *rest, part):
    o_ref, buf_ref, sems = rest[-3:]
    width, _, cols = buf_ref.shape
    loads = [
        pltpu.make_async_copy(x_ref.at[table_ref[width + j]], buf_ref.at[j], sems.at[0, j])
        for j in range(width)
    ]
    stores = [
        pltpu.make_async_copy(
            buf_ref.at[j], o_ref.at[j, :, pl.ds(part * cols, cols)], sems.at[1, j]
        )
        for j in range(width)
    ]
    for load in loads:
        load.start()
    for load, store in zip(loads, stores):
        load.wait()
        store.start()
    for store in stores:
        store.wait()


def gathered(table, returned, width, parts, part, filled):
    _, size, cols = returned.shape
    hbm = pl.BlockSpec(memory_space=pl.ANY)
    more = [] if filled is None else [filled]
    return pl.pallas_call(
        functools.partial(gather_kernel, part=part),
        out_shape=jax.ShapeDtypeStruct((width, size, cols * parts), BF16),
        in_specs=[pl.BlockSpec(memory_space=pltpu.SMEM), hbm] + [hbm] * len(more),
        out_specs=hbm,
        scratch_shapes=[
            pltpu.VMEM((width, size, cols), BF16),
            pltpu.SemaphoreType.DMA((2, width)),
        ],
        input_output_aliases={2: 0} if more else {},
    )(table, returned, *more)


def exchange(value):
    return lax.all_to_all(value, "sec", split_axis=0, concat_axis=0, tiled=True)


PARTS = 2


def on_device(
    wave_block, left_envs, next_vectors, site_weights, kept_counts, slots_before, slots_after
):
    devices = lax.axis_size("sec")
    width = left_envs.shape[1]
    env = passed_along(left_envs[0], "seg", 1)
    where = jnp.stack([lax.axis_index("sec"), lax.axis_index("seg")]).astype(jnp.int32)
    place, table, packs = prologue(
        where, slots_before, slots_after, kept_counts, next_vectors[0], devices, PARTS
    )
    arrived = []
    for h in range(PARTS):
        arrived.append(exchange(packs[h]))
    partial = partial_grams(place, wave_block[0], width)
    grams = exchange(partial)
    right, left = inverse_factors(table, grams, width, wave_block.shape[1] * devices)
    filled = None
    results = []
    for h in range(PARTS):
        result, *saved = matvec(table, arrived[h], env, site_weights[0], right, left, h)
        env = saved[0] if saved else env
        results.append(exchange(result))
    for h in range(PARTS):
        filled = gathered(table, results[h], width, PARTS, h, filled)
    return filled[None]


def solution(mesh):
    placed = (
        P("seg", "sec", None, None),
        P("seg", "sec", None, None, None),
        P("seg", "sec", None, None),
        P("seg", None, None),
        P(),
        P(),
        P(),
    )
    return jax.shard_map(
        on_device,
        mesh=mesh,
        in_specs=placed,
        out_specs=P("seg", "sec", None, None),
        check_vma=False,
    )
```

```python
import functools

import jax
import jax.numpy as jnp
from jax import lax
from jax.experimental import pallas as pl
from jax.experimental.pallas import tpu as pltpu
from jax.sharding import PartitionSpec as P


F32 = jnp.float32
BF16 = jnp.bfloat16
SIDE = 4
PARTS = 2


def passed_along(value, axis, steps):
    count = lax.axis_size(axis)
    first, last = (max(0, -steps), min(count, count - steps))
    return lax.ppermute(value, axis, [(source, source + steps) for source in range(first, last)])


def iota2(shape, axis):
    return lax.broadcasted_iota(jnp.int32, shape, axis)


def own_place(table_ref, width):
    mine = table_ref[3 * width]
    return mine // SIDE, mine % SIDE


def front_kernel(
    where_ref, before_ref, after_ref, kept_ref, vec_ref, x_ref, table_ref, *rest, width, parts
):
    packs, outs = rest[:parts], rest[parts : parts + 2 * SIDE]
    place_ref, inv_ref, vec_buf, o_ref, diag_ref, load_sem, pack_sems, sems = rest[parts + 2 * SIDE :]
    step = pl.program_id(0)
    last = pl.num_programs(0) - 1
    count, size = x_ref.shape[1:]
    half = size // 2
    each = width // 2
    cols = vec_buf.shape[2] // parts
    base = where_ref[0] * width
    mine_y, mine_x = where_ref[0] // SIDE, where_ref[0] % SIDE
    load = pltpu.make_async_copy(vec_ref, vec_buf, load_sem)

    def pack(j, h):
        return pltpu.make_async_copy(
            vec_buf.at[j, :, pl.ds(h * cols, cols)],
            packs[h].at[table_ref[width + j]],
            pack_sems.at[h, j],
        )

    @pl.when(step == 0)
    def _():
        load.start()
        diag_ref[...] = jnp.zeros_like(diag_ref)

        def invert(i, carry):
            place_ref[before_ref[i]] = i
            inv_ref[after_ref[i]] = i
            return carry

        lax.fori_loop(0, before_ref.shape[0], invert, 0)
        for j in range(width):
            sector = before_ref[base + j]
            table_ref[j] = inv_ref[sector] // width
            table_ref[width + j] = place_ref[after_ref[base + j]] // width
            table_ref[2 * width + j] = kept_ref[sector]
            table_ref[3 * width + j] = where_ref[j % 2]

    @pl.when(step == 1)
    def _():
        load.wait()
        for h in range(parts):
            for j in range(width):
                pack(j, h).start()

    turned = jnp.swapaxes(x_ref[...], 0, 1)
    row, lane = iota2((half, size), 0), iota2((half, size), 1)
    from_top = (lane >= half) & (row >= lane - half)
    on_diag = iota2((size, size), 0) == iota2((size, size), 1)
    for k in range(count):
        block = turned[k]
        full = lax.dot_general(
            block, block, (((0,), (0,)), ((), ())), preferred_element_type=F32
        )
        at = place_ref[step * count + k]
        to, slot = at // width, at % width
        colour, spot = slot // each, slot % each
        to_y, to_x = to // SIDE, to % SIDE
        along = jnp.where(colour == 0, to_x - mine_x + SIDE, to_y - mine_y + SIDE) % SIDE
        other = jnp.where(colour == 0, to_y, to_x)
        group = (colour * SIDE + along) * SIDE + other
        packed = jnp.where(from_top, pltpu.roll(full[:half], half, 1), full[half:])
        o_ref[group, pl.ds(pl.multiple_of(spot * half, half), half), :] = packed.astype(BF16)
        diag_ref[pl.ds(group * 8 + spot, 1), :] = jnp.sum(
            jnp.where(on_diag, full, 0.0), axis=0, keepdims=True
        )

    @pl.when(step == last)
    def _():
        copies = []
        for n, out in enumerate(outs):
            for m in range(n * SIDE, (n + 1) * SIDE):
                o_ref[m, each * half :, :] = two_halves(diag_ref[m * 8 : m * 8 + 8, :])
            copy = pltpu.make_async_copy(o_ref.at[pl.ds(n * SIDE, SIDE)], out, sems.at[n])
            copy.start()
            copies.append(copy)
        for h in range(parts):
            for j in range(width):
                pack(j, h).wait()
        for copy in copies:
            copy.wait()


def two_halves(exact):
    high = exact.astype(BF16).astype(F32)
    return jnp.concatenate([high, exact - high], axis=0).astype(BF16)


def front(where, before, after, kept, vectors, rows, parts, count=32):
    length, sectors, size = rows.shape
    width, _, cols = vectors.shape
    devices = sectors // width
    deep = (width // 2) * (size // 2) + 16
    hbm = pl.BlockSpec(memory_space=pl.ANY)
    table, *outs = pl.pallas_call(
        functools.partial(front_kernel, width=width, parts=parts),
        out_shape=[jax.ShapeDtypeStruct((4 * width,), jnp.int32)]
        + [jax.ShapeDtypeStruct((devices, size, cols // parts), BF16)] * parts
        + [jax.ShapeDtypeStruct((SIDE, deep, size), BF16)] * (2 * SIDE),
        grid_spec=pltpu.PrefetchScalarGridSpec(
            num_scalar_prefetch=4,
            grid=(sectors // count,),
            in_specs=[hbm, pl.BlockSpec((length, count, size), lambda i, *_: (0, i, 0))],
            out_specs=[pl.BlockSpec(memory_space=pltpu.SMEM)] + [hbm] * (parts + 2 * SIDE),
            scratch_shapes=[
                pltpu.SMEM((sectors,), jnp.int32),
                pltpu.SMEM((sectors,), jnp.int32),
                pltpu.VMEM(vectors.shape, BF16),
                pltpu.VMEM((2 * devices, deep, size), BF16),
                pltpu.VMEM((2 * devices * 8, size), F32),
                pltpu.SemaphoreType.DMA,
                pltpu.SemaphoreType.DMA((parts, width)),
                pltpu.SemaphoreType.DMA((2 * SIDE,)),
            ],
        ),
        name="front",
    )(where, before, after, kept, vectors, rows)
    return table, outs[:parts], outs[parts : parts + SIDE], outs[parts + SIDE :]


def added(parts):
    total = parts[0].astype(F32)
    for part in parts[1:]:
        total = total + part.astype(F32)
    return total


def sums_kernel(table_ref, *refs, width):
    mine = own_place(table_ref, width)
    for colour in range(2):
        ins = refs[colour * SIDE : (colour + 1) * SIDE]
        outs = refs[(2 + colour) * SIDE : (3 + colour) * SIDE]
        for along, out in enumerate(outs):
            at = (mine[colour] + along) % SIDE
            total = added([ref[at] for ref in ins])
            tail = total.shape[0] - 16
            out[:tail] = total[:tail].astype(BF16)
            out[tail:] = two_halves(total[tail : tail + 8] + total[tail + 8 :])


def axis_sums(table, first, second, width):
    _, deep, size = first[0].shape
    vmem = pl.BlockSpec(memory_space=pltpu.VMEM)
    outs = pl.pallas_call(
        functools.partial(sums_kernel, width=width),
        out_shape=[jax.ShapeDtypeStruct((deep, size), BF16)] * (2 * SIDE),
        in_specs=[pl.BlockSpec(memory_space=pltpu.SMEM)] + [vmem] * (2 * SIDE),
        out_specs=[vmem] * (2 * SIDE),
        name="sums",
    )(table, *first, *second)
    return outs[:SIDE], outs[SIDE:]


def turned_round(parts, axis):
    moved = [parts[0]]
    for along in range(1, SIDE):
        pairs = []
        for y in range(SIDE):
            for x in range(SIDE):
                to = (y, (x + along) % SIDE) if axis == "x" else ((y + along) % SIDE, x)
                pairs.append((y * SIDE + x, to[0] * SIDE + to[1]))
        moved.append(lax.ppermute(parts[along], "sec", pairs))
    return moved


def split3(value):
    high = value.astype(BF16)
    rest = value - high.astype(F32)
    mid = rest.astype(BF16)
    low = (rest - mid.astype(F32)).astype(BF16)
    return high, mid, low


def factor_kernel(table_ref, *refs, total_rows):
    right_ref, left_ref, state_ref = refs[-3:]
    width, size, _ = state_ref.shape
    half = size // 2
    each = width // 2
    scale = 1.0 / total_rows
    packed, diag = [], []
    for colour in range(2):
        total = added([ref[...] for ref in refs[colour * SIDE : (colour + 1) * SIDE]]) * scale
        tail = each * half
        exact = total[tail : tail + 8] + total[tail + 8 :]
        for m in range(each):
            packed.append(total[m * half : (m + 1) * half])
            diag.append(exact[m : m + 1])
    lane = iota2((half, size), 1)
    row2, lane2 = iota2((size, size), 0), iota2((size, size), 1)
    for m in range(width):
        p = packed[m]
        turned = jnp.concatenate([p, p], axis=0).T
        top = jnp.where(lane >= half, turned[:half], pltpu.roll(turned[half:], half, 1))
        upper = jnp.concatenate([top, p], axis=0)
        both = jnp.where(lane2 > row2, upper, upper.T)
        state_ref[m] = jnp.where(lane2 == row2, diag[m] + 0.1, both)

    lane8, sub8 = iota2((8, size), 1), iota2((8, size), 0)
    for r0 in range(0, size, 8):
        panel = state_ref[:, r0 : r0 + 8, :]
        for k in range(8):
            c = r0 + k
            col = panel[:, :, c : c + 1]
            pivot = panel[:, k : k + 1, c : c + 1]
            rk = lax.rsqrt(pivot)
            rk = rk * (1.5 - 0.5 * pivot * rk * rk)
            lead = jnp.where(lane8[:1] == c, rk, panel[:, k : k + 1, :] * rk)
            kept = jnp.where(lane8 == c, 0.0, panel) - (col * rk) * lead
            panel = jnp.where(sub8 > k, kept, jnp.where(sub8 == k, lead, panel))
        rest = r0 + 8
        panel = jnp.where((lane8 < rest) & (lane8 > r0 + sub8), 0.0, panel)
        state_ref[:, r0:rest, :] = panel
        if rest < size:
            h, m_, l = split3(panel)
            one = jnp.concatenate([h, h, h, m_, m_, l], axis=1)
            two = jnp.concatenate([h, m_, l, h, m_, h], axis=1)
            inside = (lane2[rest:] >= r0) & (lane2[rest:] < rest)
            for m in range(width):
                update = lax.dot_general(
                    one[m], two[m], (((0,), (0,)), ((), ())), preferred_element_type=F32
                )
                old = jnp.where(inside, 0.0, state_ref[m, rest:, :])
                state_ref[m, rest:, :] = old - update[rest:]

    for m in range(width):
        inverse = jnp.where(
            (lane2 <= row2) & (row2 < table_ref[2 * width + m]), state_ref[m], 0.0
        )
        high, low, _ = split3(inverse)
        left_ref[m] = jnp.concatenate([high, low, high], axis=1)
        high, low, _ = split3(inverse.T)
        right_ref[m] = jnp.concatenate([high, low], axis=1)


def inverse_factors(table, first, second, width, total_rows):
    size = first[0].shape[1]
    shapes = ((width, size, 2 * size), (width, size, 3 * size))
    vmem = pl.BlockSpec(memory_space=pltpu.VMEM)
    return pl.pallas_call(
        functools.partial(factor_kernel, total_rows=total_rows),
        out_shape=tuple(jax.ShapeDtypeStruct(s, BF16) for s in shapes),
        in_specs=[pl.BlockSpec(memory_space=pltpu.SMEM)] + [vmem] * (2 * SIDE),
        out_specs=(vmem, vmem),
        scratch_shapes=[pltpu.VMEM((width, size, size), F32)],
        name="factor",
    )(table, *first, *second)


def matvec_kernel(table_ref, v_ref, e_ref, w_ref, right_ref, left_ref, *rest, part, group):
    if part:
        _, o_ref, v_buf, wide_buf, y_buf, o_buf, sems = rest
    else:
        o_ref, wide_ref, v_buf, e_buf, wide_buf, y_buf, o_buf, sems = rest
    width, size, cols = v_buf.shape
    channels = w_ref.shape[0]
    span = pl.ds(part * cols, cols)
    copy = pltpu.make_async_copy
    v_in = [copy(v_ref.at[table_ref[i]], v_buf.at[i], sems.at[0, i]) for i in range(width)]
    e_to = wide_buf if part else e_buf
    e_in = [copy(e_ref.at[i], e_to.at[i], sems.at[1, i]) for i in range(width)]
    outs = [
        copy(o_buf.at[i], o_ref.at[table_ref[i], :, span], sems.at[2, i]) for i in range(width)
    ]
    for load in v_in + e_in:
        load.start()
    for i in range(width):
        v_in[i].wait()
        v = v_buf[i]
        y_buf[i] = jnp.dot(
            right_ref[i], jnp.concatenate([v, v], axis=0), preferred_element_type=F32
        )
    saves = []
    if not part:
        eye = (iota2((size, size), 0) == iota2((size, size), 1)).astype(BF16)
        first = table_ref[3 * width + 1] == 0

    def ready(i):
        e_in[i].wait()
        if part:
            return
        env = jnp.swapaxes(e_buf[i], 0, 1)
        for u in range(channels):
            alone = eye if u == 0 else jnp.zeros_like(eye)
            wide_buf[i, :, u * size : (u + 1) * size] = jnp.where(first, alone, env[u])
        saves.append(copy(wide_buf.at[i], wide_ref.at[i], sems.at[3, i]))
        saves[-1].start()

    def mixed(i):
        y = y_buf[i]
        total = None
        for w in range(0, channels, group):
            scaled = [
                (y * w_ref[u : u + 1, span]).astype(BF16) for u in range(w, w + group)
            ]
            piece = jnp.dot(
                wide_buf[i, :, w * size : (w + group) * size],
                jnp.concatenate(scaled, axis=0),
                preferred_element_type=F32,
            )
            total = piece if total is None else total + piece
        return total

    def finish(i, total):
        high = total.astype(BF16)
        low = (total - high.astype(F32)).astype(BF16)
        o_buf[i] = jnp.dot(
            left_ref[i], jnp.concatenate([high, high, low], axis=0), preferred_element_type=F32
        ).astype(BF16)
        outs[i].start()

    ready(0)
    before = None
    for i in range(width):
        if i + 1 < width:
            ready(i + 1)
        total = mixed(i)
        if i:
            finish(i - 1, before)
        before = total
    finish(width - 1, before)
    for out in outs + saves:
        out.wait()


def matvec(table, arrived, env, weights, right, left, part, filled, group=4):
    width, size, _ = right.shape
    channels, all_cols = weights.shape
    devices, _, cols = arrived.shape
    hbm = pl.BlockSpec(memory_space=pl.ANY)
    vmem = pl.BlockSpec(memory_space=pltpu.VMEM)
    out_shape = [jax.ShapeDtypeStruct((devices, size, all_cols), BF16)]
    wide = (width, size, channels * size)
    scratch = [pltpu.VMEM((width, size, cols), BF16)]
    if part == 0:
        out_shape.append(jax.ShapeDtypeStruct(wide, BF16))
        scratch.append(pltpu.VMEM(env.shape, BF16))
    scratch += [
        pltpu.VMEM(wide, BF16),
        pltpu.VMEM((width, size, cols), F32),
        pltpu.VMEM((width, size, cols), BF16),
        pltpu.SemaphoreType.DMA((4, width)),
    ]
    more = [] if part == 0 else [filled]
    return pl.pallas_call(
        functools.partial(matvec_kernel, part=part, group=group),
        out_shape=out_shape,
        in_specs=[pl.BlockSpec(memory_space=pltpu.SMEM), hbm, hbm, vmem, vmem, vmem]
        + [hbm] * len(more),
        out_specs=[hbm] * len(out_shape),
        scratch_shapes=scratch,
        input_output_aliases={6: 0} if more else {},
    )(table, arrived, env, weights, right, left, *more)


def gather_kernel(table_ref, x_ref, o_ref, buf_ref, sems):
    width = buf_ref.shape[0]
    loads = [
        pltpu.make_async_copy(x_ref.at[table_ref[width + j]], buf_ref.at[j], sems.at[0, j])
        for j in range(width)
    ]
    stores = [
        pltpu.make_async_copy(buf_ref.at[j], o_ref.at[j], sems.at[1, j]) for j in range(width)
    ]
    for load in loads:
        load.start()
    for load, store in zip(loads, stores):
        load.wait()
        store.start()
    for store in stores:
        store.wait()


def gathered(table, returned, width):
    _, size, cols = returned.shape
    hbm = pl.BlockSpec(memory_space=pl.ANY)
    shape = (width, size, cols)
    return pl.pallas_call(
        gather_kernel,
        out_shape=jax.ShapeDtypeStruct(shape, BF16),
        in_specs=[pl.BlockSpec(memory_space=pltpu.SMEM), hbm],
        out_specs=hbm,
        scratch_shapes=[pltpu.VMEM(shape, BF16), pltpu.SemaphoreType.DMA((2, width))],
        name="gather",
    )(table, returned)


def exchange(value):
    return lax.all_to_all(value, "sec", split_axis=0, concat_axis=0, tiled=True)


def on_device(
    wave_block, left_envs, next_vectors, site_weights, kept_counts, slots_before, slots_after
):
    width = left_envs.shape[1]
    total_rows = wave_block.shape[1] * lax.axis_size("sec")
    env = passed_along(left_envs[0], "seg", 1)
    where = jnp.stack([lax.axis_index("sec"), lax.axis_index("seg")]).astype(jnp.int32)
    table, packs, first, second = front(
        where, slots_before, slots_after, kept_counts, next_vectors[0], wave_block[0], PARTS
    )
    arrived = []
    for h in range(PARTS):
        arrived.append(exchange(packs[h]))
    first, second = turned_round(first, "x"), turned_round(second, "y")
    first, second = axis_sums(table, first, second, width)
    first, second = turned_round(first, "y"), turned_round(second, "x")
    right, left = inverse_factors(table, first, second, width, total_rows)
    result = None
    for h in range(PARTS):
        result, *wide = matvec(
            table, arrived[h], env, site_weights[0], right, left, h, result
        )
        env = wide[0] if wide else env
    returned = exchange(result)
    return gathered(table, returned, width)[None]


def solution(mesh):
    placed = (
        P("seg", "sec", None, None),
        P("seg", "sec", None, None, None),
        P("seg", "sec", None, None),
        P("seg", None, None),
        P(),
        P(),
        P(),
    )
    return jax.shard_map(
        on_device,
        mesh=mesh,
        in_specs=placed,
        out_specs=P("seg", "sec", None, None),
        check_vma=False,
    )
```

```python
import functools

import jax
import jax.numpy as jnp
from jax import lax
from jax.experimental import pallas as pl
from jax.experimental.pallas import tpu as pltpu
from jax.sharding import PartitionSpec as P


F32 = jnp.float32
BF16 = jnp.bfloat16
SIDE = 4
PARTS = 2


def passed_along(value, axis, steps):
    count = lax.axis_size(axis)
    first, last = (max(0, -steps), min(count, count - steps))
    return lax.ppermute(value, axis, [(source, source + steps) for source in range(first, last)])


def iota2(shape, axis):
    return lax.broadcasted_iota(jnp.int32, shape, axis)


def own_place(table_ref, width):
    mine = table_ref[3 * width]
    return mine // SIDE, mine % SIDE


def front_kernel(
    where_ref, before_ref, after_ref, kept_ref, vec_ref, x_ref, table_ref, *rest, width, parts
):
    packs, outs = rest[:parts], rest[parts : parts + 2 * SIDE]
    place_ref, inv_ref, vec_buf, o_ref, diag_ref, load_sem, pack_sems, sems = rest[parts + 2 * SIDE :]
    step = pl.program_id(0)
    last = pl.num_programs(0) - 1
    count, size = x_ref.shape[1:]
    half = size // 2
    each = width // 2
    cols = vec_buf.shape[2] // parts
    base = where_ref[0] * width
    mine_y, mine_x = where_ref[0] // SIDE, where_ref[0] % SIDE
    load = pltpu.make_async_copy(vec_ref, vec_buf, load_sem)

    def pack(j, h):
        return pltpu.make_async_copy(
            vec_buf.at[j, :, pl.ds(h * cols, cols)],
            packs[h].at[table_ref[width + j]],
            pack_sems.at[h, j],
        )

    @pl.when(step == 0)
    def _():
        load.start()
        diag_ref[...] = jnp.zeros_like(diag_ref)

        def invert(i, carry):
            place_ref[before_ref[i]] = i
            inv_ref[after_ref[i]] = i
            return carry

        lax.fori_loop(0, before_ref.shape[0], invert, 0)
        for j in range(width):
            sector = before_ref[base + j]
            table_ref[j] = inv_ref[sector] // width
            table_ref[width + j] = place_ref[after_ref[base + j]] // width
            table_ref[2 * width + j] = kept_ref[sector]
            table_ref[3 * width + j] = where_ref[j % 2]

    @pl.when(step == 1)
    def _():
        load.wait()
        for h in range(parts):
            for j in range(width):
                pack(j, h).start()

    turned = jnp.swapaxes(x_ref[...], 0, 1)
    row, lane = iota2((half, size), 0), iota2((half, size), 1)
    from_top = (lane >= half) & (row >= lane - half)
    on_diag = iota2((size, size), 0) == iota2((size, size), 1)
    for k in range(count):
        block = turned[k]
        full = lax.dot_general(
            block, block, (((0,), (0,)), ((), ())), preferred_element_type=F32
        )
        at = place_ref[step * count + k]
        to, slot = at // width, at % width
        colour, spot = slot // each, slot % each
        to_y, to_x = to // SIDE, to % SIDE
        along = jnp.where(colour == 0, to_x - mine_x + SIDE, to_y - mine_y + SIDE) % SIDE
        other = jnp.where(colour == 0, to_y, to_x)
        group = (colour * SIDE + along) * SIDE + other
        packed = jnp.where(from_top, pltpu.roll(full[:half], half, 1), full[half:])
        o_ref[group, pl.ds(pl.multiple_of(spot * half, half), half), :] = packed.astype(BF16)
        diag_ref[pl.ds(group * 8 + spot, 1), :] = jnp.sum(
            jnp.where(on_diag, full, 0.0), axis=0, keepdims=True
        )

    @pl.when(step == last)
    def _():
        copies = []
        for n, out in enumerate(outs):
            for m in range(n * SIDE, (n + 1) * SIDE):
                o_ref[m, each * half :, :] = two_halves(diag_ref[m * 8 : m * 8 + 8, :])
            copy = pltpu.make_async_copy(o_ref.at[pl.ds(n * SIDE, SIDE)], out, sems.at[n])
            copy.start()
            copies.append(copy)
        for h in range(parts):
            for j in range(width):
                pack(j, h).wait()
        for copy in copies:
            copy.wait()


def two_halves(exact):
    high = exact.astype(BF16).astype(F32)
    return jnp.concatenate([high, exact - high], axis=0).astype(BF16)


def front(where, before, after, kept, vectors, rows, parts, count=32):
    length, sectors, size = rows.shape
    width, _, cols = vectors.shape
    devices = sectors // width
    deep = (width // 2) * (size // 2) + 16
    hbm = pl.BlockSpec(memory_space=pl.ANY)
    table, *outs = pl.pallas_call(
        functools.partial(front_kernel, width=width, parts=parts),
        out_shape=[jax.ShapeDtypeStruct((4 * width,), jnp.int32)]
        + [jax.ShapeDtypeStruct((devices, size, cols // parts), BF16)] * parts
        + [jax.ShapeDtypeStruct((SIDE, deep, size), BF16)] * (2 * SIDE),
        grid_spec=pltpu.PrefetchScalarGridSpec(
            num_scalar_prefetch=4,
            grid=(sectors // count,),
            in_specs=[hbm, pl.BlockSpec((length, count, size), lambda i, *_: (0, i, 0))],
            out_specs=[pl.BlockSpec(memory_space=pltpu.SMEM)] + [hbm] * (parts + 2 * SIDE),
            scratch_shapes=[
                pltpu.SMEM((sectors,), jnp.int32),
                pltpu.SMEM((sectors,), jnp.int32),
                pltpu.VMEM(vectors.shape, BF16),
                pltpu.VMEM((2 * devices, deep, size), BF16),
                pltpu.VMEM((2 * devices * 8, size), F32),
                pltpu.SemaphoreType.DMA,
                pltpu.SemaphoreType.DMA((parts, width)),
                pltpu.SemaphoreType.DMA((2 * SIDE,)),
            ],
        ),
        name="front",
    )(where, before, after, kept, vectors, rows)
    return table, outs[:parts], outs[parts : parts + SIDE], outs[parts + SIDE :]


def added(parts):
    total = parts[0].astype(F32)
    for part in parts[1:]:
        total = total + part.astype(F32)
    return total


def sums_kernel(table_ref, *refs, width):
    mine = own_place(table_ref, width)
    for colour in range(2):
        ins = refs[colour * SIDE : (colour + 1) * SIDE]
        outs = refs[(2 + colour) * SIDE : (3 + colour) * SIDE]
        for along, out in enumerate(outs):
            at = (mine[colour] + along) % SIDE
            total = added([ref[at] for ref in ins])
            tail = total.shape[0] - 16
            out[:tail] = total[:tail].astype(BF16)
            out[tail:] = two_halves(total[tail : tail + 8] + total[tail + 8 :])


def axis_sums(table, first, second, width):
    _, deep, size = first[0].shape
    vmem = pl.BlockSpec(memory_space=pltpu.VMEM)
    outs = pl.pallas_call(
        functools.partial(sums_kernel, width=width),
        out_shape=[jax.ShapeDtypeStruct((deep, size), BF16)] * (2 * SIDE),
        in_specs=[pl.BlockSpec(memory_space=pltpu.SMEM)] + [vmem] * (2 * SIDE),
        out_specs=[vmem] * (2 * SIDE),
        name="sums",
    )(table, *first, *second)
    return outs[:SIDE], outs[SIDE:]


def turned_round(parts, axis):
    moved = [parts[0]]
    for along in range(1, SIDE):
        pairs = []
        for y in range(SIDE):
            for x in range(SIDE):
                to = (y, (x + along) % SIDE) if axis == "x" else ((y + along) % SIDE, x)
                pairs.append((y * SIDE + x, to[0] * SIDE + to[1]))
        moved.append(lax.ppermute(parts[along], "sec", pairs))
    return moved


def split3(value):
    high = value.astype(BF16)
    rest = value - high.astype(F32)
    mid = rest.astype(BF16)
    low = (rest - mid.astype(F32)).astype(BF16)
    return high, mid, low


def factor_kernel(table_ref, *refs, total_rows):
    right_ref, left_ref, state_ref = refs[-3:]
    width, size, _ = state_ref.shape
    half = size // 2
    each = width // 2
    scale = 1.0 / total_rows
    packed, diag = [], []
    for colour in range(2):
        total = added([ref[...] for ref in refs[colour * SIDE : (colour + 1) * SIDE]]) * scale
        tail = each * half
        exact = total[tail : tail + 8] + total[tail + 8 :]
        for m in range(each):
            packed.append(total[m * half : (m + 1) * half])
            diag.append(exact[m : m + 1])
    lane = iota2((half, size), 1)
    row2, lane2 = iota2((size, size), 0), iota2((size, size), 1)
    for m in range(width):
        p = packed[m]
        turned = jnp.concatenate([p, p], axis=0).T
        top = jnp.where(lane >= half, turned[:half], pltpu.roll(turned[half:], half, 1))
        upper = jnp.concatenate([top, p], axis=0)
        both = jnp.where(lane2 > row2, upper, upper.T)
        state_ref[m] = jnp.where(lane2 == row2, diag[m] + 0.1, both)

    deep = 16
    lanes, subs = iota2((deep, size), 1), iota2((deep, size), 0)
    for r0 in range(0, size, deep):
        panel = state_ref[:, r0 : r0 + deep, :]
        for k in range(deep):
            c = r0 + k
            col = panel[:, :, c : c + 1]
            pivot = panel[:, k : k + 1, c : c + 1]
            rk = lax.rsqrt(pivot)
            lead = jnp.where(lanes[:1] == c, rk, panel[:, k : k + 1, :] * rk)
            kept = jnp.where(lanes == c, 0.0, panel) - (col * rk) * lead
            panel = jnp.where(subs > k, kept, jnp.where(subs == k, lead, panel))
        rest = r0 + deep
        panel = jnp.where((lanes < rest) & (lanes > r0 + subs), 0.0, panel)
        state_ref[:, r0:rest, :] = panel
        if rest < size:
            h, m_, l = split3(panel)
            one = jnp.concatenate([h, h, h, m_, m_, l], axis=1)
            two = jnp.concatenate([h, m_, l, h, m_, h], axis=1)
            inside = (lane2[rest:] >= r0) & (lane2[rest:] < rest)
            for m in range(width):
                update = lax.dot_general(
                    one[m], two[m], (((0,), (0,)), ((), ())), preferred_element_type=F32
                )
                old = jnp.where(inside, 0.0, state_ref[m, rest:, :])
                state_ref[m, rest:, :] = old - update[rest:]

    for m in range(width):
        inverse = jnp.where(
            (lane2 <= row2) & (row2 < table_ref[2 * width + m]), state_ref[m], 0.0
        )
        high, low, _ = split3(inverse)
        left_ref[m] = jnp.concatenate([high, low, high], axis=1)
        high, low, _ = split3(inverse.T)
        right_ref[m] = jnp.concatenate([high, low], axis=1)


def inverse_factors(table, first, second, width, total_rows):
    size = first[0].shape[1]
    shapes = ((width, size, 2 * size), (width, size, 3 * size))
    vmem = pl.BlockSpec(memory_space=pltpu.VMEM)
    return pl.pallas_call(
        functools.partial(factor_kernel, total_rows=total_rows),
        out_shape=tuple(jax.ShapeDtypeStruct(s, BF16) for s in shapes),
        in_specs=[pl.BlockSpec(memory_space=pltpu.SMEM)] + [vmem] * (2 * SIDE),
        out_specs=(vmem, vmem),
        scratch_shapes=[pltpu.VMEM((width, size, size), F32)],
        name="factor",
    )(table, *first, *second)


def matvec_kernel(table_ref, v_ref, e_ref, w_ref, right_ref, left_ref, *rest, part, group):
    if part:
        _, o_ref, v_buf, wide_buf, y_buf, o_buf, sems = rest
    else:
        o_ref, wide_ref, v_buf, e_buf, wide_buf, y_buf, o_buf, sems = rest
    width, size, cols = v_buf.shape
    channels = w_ref.shape[0]
    span = pl.ds(part * cols, cols)
    copy = pltpu.make_async_copy
    v_in = [copy(v_ref.at[table_ref[i]], v_buf.at[i], sems.at[0, i]) for i in range(width)]
    e_to = wide_buf if part else e_buf
    e_in = [copy(e_ref.at[i], e_to.at[i], sems.at[1, i]) for i in range(width)]
    outs = [
        copy(o_buf.at[i], o_ref.at[table_ref[i], :, span], sems.at[2, i]) for i in range(width)
    ]
    for load in v_in + e_in:
        load.start()
    for i in range(width):
        v_in[i].wait()
        v = v_buf[i]
        y_buf[i] = jnp.dot(
            right_ref[i], jnp.concatenate([v, v], axis=0), preferred_element_type=F32
        )
    saves = []
    if not part:
        eye = (iota2((size, size), 0) == iota2((size, size), 1)).astype(BF16)
        first = table_ref[3 * width + 1] == 0

    def ready(i):
        e_in[i].wait()
        if part:
            return
        env = jnp.swapaxes(e_buf[i], 0, 1)
        for u in range(channels):
            block = jnp.where(first, eye, env[u]) if u == 0 else env[u]
            wide_buf[i, :, u * size : (u + 1) * size] = block
        saves.append(copy(wide_buf.at[i], wide_ref.at[i], sems.at[3, i]))
        saves[-1].start()

    def mixed(i):
        y = y_buf[i]
        total = None
        for w in range(0, channels, group):
            scaled = [
                (y * w_ref[u : u + 1, span]).astype(BF16) for u in range(w, w + group)
            ]
            piece = jnp.dot(
                wide_buf[i, :, w * size : (w + group) * size],
                jnp.concatenate(scaled, axis=0),
                preferred_element_type=F32,
            )
            total = piece if total is None else total + piece
        return total

    def finish(i, total):
        high = total.astype(BF16)
        low = (total - high.astype(F32)).astype(BF16)
        o_buf[i] = jnp.dot(
            left_ref[i], jnp.concatenate([high, high, low], axis=0), preferred_element_type=F32
        ).astype(BF16)
        outs[i].start()

    ready(0)
    before = None
    for i in range(width):
        if i + 1 < width:
            ready(i + 1)
        total = mixed(i)
        if i:
            finish(i - 1, before)
        before = total
    finish(width - 1, before)
    for out in outs + saves:
        out.wait()


def matvec(table, arrived, env, weights, right, left, part, filled, group=4):
    width, size, _ = right.shape
    channels, all_cols = weights.shape
    devices, _, cols = arrived.shape
    hbm = pl.BlockSpec(memory_space=pl.ANY)
    vmem = pl.BlockSpec(memory_space=pltpu.VMEM)
    out_shape = [jax.ShapeDtypeStruct((devices, size, all_cols), BF16)]
    wide = (width, size, channels * size)
    scratch = [pltpu.VMEM((width, size, cols), BF16)]
    if part == 0:
        out_shape.append(jax.ShapeDtypeStruct(wide, BF16))
        scratch.append(pltpu.VMEM(env.shape, BF16))
    scratch += [
        pltpu.VMEM(wide, BF16),
        pltpu.VMEM((width, size, cols), F32),
        pltpu.VMEM((width, size, cols), BF16),
        pltpu.SemaphoreType.DMA((4, width)),
    ]
    more = [] if part == 0 else [filled]
    return pl.pallas_call(
        functools.partial(matvec_kernel, part=part, group=group),
        out_shape=out_shape,
        in_specs=[pl.BlockSpec(memory_space=pltpu.SMEM), hbm, hbm, vmem, vmem, vmem]
        + [hbm] * len(more),
        out_specs=[hbm] * len(out_shape),
        scratch_shapes=scratch,
        input_output_aliases={6: 0} if more else {},
    )(table, arrived, env, weights, right, left, *more)


def gather_kernel(table_ref, x_ref, o_ref, buf_ref, sems):
    width = buf_ref.shape[0]
    loads = [
        pltpu.make_async_copy(x_ref.at[table_ref[width + j]], buf_ref.at[j], sems.at[0, j])
        for j in range(width)
    ]
    stores = [
        pltpu.make_async_copy(buf_ref.at[j], o_ref.at[j], sems.at[1, j]) for j in range(width)
    ]
    for load in loads:
        load.start()
    for load, store in zip(loads, stores):
        load.wait()
        store.start()
    for store in stores:
        store.wait()


def gathered(table, returned, width):
    _, size, cols = returned.shape
    hbm = pl.BlockSpec(memory_space=pl.ANY)
    shape = (width, size, cols)
    return pl.pallas_call(
        gather_kernel,
        out_shape=jax.ShapeDtypeStruct(shape, BF16),
        in_specs=[pl.BlockSpec(memory_space=pltpu.SMEM), hbm],
        out_specs=hbm,
        scratch_shapes=[pltpu.VMEM(shape, BF16), pltpu.SemaphoreType.DMA((2, width))],
        name="gather",
    )(table, returned)


def exchange(value):
    return lax.all_to_all(value, "sec", split_axis=0, concat_axis=0, tiled=True)


def on_device(
    wave_block, left_envs, next_vectors, site_weights, kept_counts, slots_before, slots_after
):
    width = left_envs.shape[1]
    total_rows = wave_block.shape[1] * lax.axis_size("sec")
    env = passed_along(left_envs[0], "seg", 1)
    where = jnp.stack([lax.axis_index("sec"), lax.axis_index("seg")]).astype(jnp.int32)
    table, packs, first, second = front(
        where, slots_before, slots_after, kept_counts, next_vectors[0], wave_block[0], PARTS
    )
    arrived = []
    for h in range(PARTS):
        arrived.append(exchange(packs[h]))
    first, second = turned_round(first, "x"), turned_round(second, "y")
    first, second = axis_sums(table, first, second, width)
    first, second = turned_round(first, "y"), turned_round(second, "x")
    right, left = inverse_factors(table, first, second, width, total_rows)
    result = None
    for h in range(PARTS):
        result, *wide = matvec(
            table, arrived[h], env, site_weights[0], right, left, h, result
        )
        env = wide[0] if wide else env
    returned = exchange(result)
    return gathered(table, returned, width)[None]


def solution(mesh):
    placed = (
        P("seg", "sec", None, None),
        P("seg", "sec", None, None, None),
        P("seg", "sec", None, None),
        P("seg", None, None),
        P(),
        P(),
        P(),
    )
    return jax.shard_map(
        on_device,
        mesh=mesh,
        in_specs=placed,
        out_specs=P("seg", "sec", None, None),
        check_vma=False,
    )
```

```python
import functools

import jax
import jax.numpy as jnp
from jax import lax
from jax.experimental import pallas as pl
from jax.experimental.pallas import tpu as pltpu
from jax.sharding import PartitionSpec as P


F32 = jnp.float32
BF16 = jnp.bfloat16
SIDE = 4
PARTS = 2


def passed_along(value, axis, steps):
    count = lax.axis_size(axis)
    first, last = (max(0, -steps), min(count, count - steps))
    return lax.ppermute(value, axis, [(source, source + steps) for source in range(first, last)])


def iota2(shape, axis):
    return lax.broadcasted_iota(jnp.int32, shape, axis)


def own_place(table_ref, width):
    mine = table_ref[3 * width]
    return mine // SIDE, mine % SIDE


def front_kernel(
    sec_ref, seg_ref, before_ref, after_ref, kept_ref, vec_ref, x_ref, table_ref, *rest, width, parts
):
    packs, outs = rest[:parts], rest[parts : parts + 2 * SIDE]
    place_ref, inv_ref, vec_buf, o_ref, diag_ref, load_sem, pack_sems, sems = rest[parts + 2 * SIDE :]
    step = pl.program_id(0)
    last = pl.num_programs(0) - 1
    count, size = x_ref.shape[1:]
    half = size // 2
    each = width // 2
    cols = vec_buf.shape[2] // parts
    base = sec_ref[0] * width
    mine_y, mine_x = sec_ref[0] // SIDE, sec_ref[0] % SIDE
    load = pltpu.make_async_copy(vec_ref, vec_buf, load_sem)

    def pack(j, h):
        return pltpu.make_async_copy(
            vec_buf.at[j, :, pl.ds(h * cols, cols)],
            packs[h].at[table_ref[width + j]],
            pack_sems.at[h, j],
        )

    @pl.when(step == 0)
    def _():
        load.start()
        diag_ref[...] = jnp.zeros_like(diag_ref)

        def invert(i, carry):
            place_ref[before_ref[i]] = i
            inv_ref[after_ref[i]] = i
            return carry

        lax.fori_loop(0, before_ref.shape[0], invert, 0, unroll=8)
        for j in range(width):
            sector = before_ref[base + j]
            table_ref[j] = inv_ref[sector] // width
            table_ref[width + j] = place_ref[after_ref[base + j]] // width
            table_ref[2 * width + j] = kept_ref[sector]
            table_ref[3 * width + j] = seg_ref[0] if j % 2 else sec_ref[0]

    @pl.when(step == 1)
    def _():
        load.wait()
        for h in range(parts):
            for j in range(width):
                pack(j, h).start()

    turned = jnp.swapaxes(x_ref[...], 0, 1)
    row, lane = iota2((half, size), 0), iota2((half, size), 1)
    from_top = (lane >= half) & (row >= lane - half)
    on_diag = iota2((size, size), 0) == iota2((size, size), 1)
    for k in range(count):
        block = turned[k]
        full = lax.dot_general(
            block, block, (((0,), (0,)), ((), ())), preferred_element_type=F32
        )
        at = place_ref[step * count + k]
        to, slot = at // width, at % width
        colour, spot = slot // each, slot % each
        to_y, to_x = to // SIDE, to % SIDE
        along = jnp.where(colour == 0, to_x - mine_x + SIDE, to_y - mine_y + SIDE) % SIDE
        other = jnp.where(colour == 0, to_y, to_x)
        group = (colour * SIDE + along) * SIDE + other
        packed = jnp.where(from_top, pltpu.roll(full[:half], half, 1), full[half:])
        o_ref[group, pl.ds(pl.multiple_of(spot * half, half), half), :] = packed.astype(BF16)
        diag_ref[pl.ds(group * 8 + spot, 1), :] = jnp.sum(
            jnp.where(on_diag, full, 0.0), axis=0, keepdims=True
        )

    @pl.when(step == last)
    def _():
        copies = []
        for n, out in enumerate(outs):
            for m in range(n * SIDE, (n + 1) * SIDE):
                o_ref[m, each * half :, :] = two_halves(diag_ref[m * 8 : m * 8 + 8, :])
            copy = pltpu.make_async_copy(o_ref.at[pl.ds(n * SIDE, SIDE)], out, sems.at[n])
            copy.start()
            copies.append(copy)
        for h in range(parts):
            for j in range(width):
                pack(j, h).wait()
        for copy in copies:
            copy.wait()


def two_halves(exact):
    high = exact.astype(BF16).astype(F32)
    return jnp.concatenate([high, exact - high], axis=0).astype(BF16)


def front(sec, seg, before, after, kept, vectors, rows, parts, count=32):
    length, sectors, size = rows.shape
    width, _, cols = vectors.shape
    devices = sectors // width
    deep = (width // 2) * (size // 2) + 16
    hbm = pl.BlockSpec(memory_space=pl.ANY)
    table, *outs = pl.pallas_call(
        functools.partial(front_kernel, width=width, parts=parts),
        out_shape=[jax.ShapeDtypeStruct((4 * width,), jnp.int32)]
        + [jax.ShapeDtypeStruct((devices, size, cols // parts), BF16)] * parts
        + [jax.ShapeDtypeStruct((SIDE, deep, size), BF16)] * (2 * SIDE),
        grid_spec=pltpu.PrefetchScalarGridSpec(
            num_scalar_prefetch=5,
            grid=(sectors // count,),
            in_specs=[hbm, pl.BlockSpec((length, count, size), lambda i, *_: (0, i, 0))],
            out_specs=[pl.BlockSpec(memory_space=pltpu.SMEM)] + [hbm] * (parts + 2 * SIDE),
            scratch_shapes=[
                pltpu.SMEM((sectors,), jnp.int32),
                pltpu.SMEM((sectors,), jnp.int32),
                pltpu.VMEM(vectors.shape, BF16),
                pltpu.VMEM((2 * devices, deep, size), BF16),
                pltpu.VMEM((2 * devices * 8, size), F32),
                pltpu.SemaphoreType.DMA,
                pltpu.SemaphoreType.DMA((parts, width)),
                pltpu.SemaphoreType.DMA((2 * SIDE,)),
            ],
        ),
        name="front",
    )(sec, seg, before, after, kept, vectors, rows)
    return table, outs[:parts], outs[parts : parts + SIDE], outs[parts + SIDE :]


def added(parts):
    total = parts[0].astype(F32)
    for part in parts[1:]:
        total = total + part.astype(F32)
    return total


def sums_kernel(table_ref, *refs, width):
    mine = own_place(table_ref, width)
    for colour in range(2):
        ins = refs[colour * SIDE : (colour + 1) * SIDE]
        outs = refs[(2 + colour) * SIDE : (3 + colour) * SIDE]
        for along, out in enumerate(outs):
            at = (mine[colour] + along) % SIDE
            total = added([ref[at] for ref in ins])
            tail = total.shape[0] - 16
            out[:tail] = total[:tail].astype(BF16)
            out[tail:] = two_halves(total[tail : tail + 8] + total[tail + 8 :])


def axis_sums(table, first, second, width):
    _, deep, size = first[0].shape
    vmem = pl.BlockSpec(memory_space=pltpu.VMEM)
    outs = pl.pallas_call(
        functools.partial(sums_kernel, width=width),
        out_shape=[jax.ShapeDtypeStruct((deep, size), BF16)] * (2 * SIDE),
        in_specs=[pl.BlockSpec(memory_space=pltpu.SMEM)] + [vmem] * (2 * SIDE),
        out_specs=[vmem] * (2 * SIDE),
        name="sums",
    )(table, *first, *second)
    return outs[:SIDE], outs[SIDE:]


def turned_round(parts, axis):
    moved = [parts[0]]
    for along in range(1, SIDE):
        pairs = []
        for y in range(SIDE):
            for x in range(SIDE):
                to = (y, (x + along) % SIDE) if axis == "x" else ((y + along) % SIDE, x)
                pairs.append((y * SIDE + x, to[0] * SIDE + to[1]))
        moved.append(lax.ppermute(parts[along], "sec", pairs))
    return moved


def split3(value):
    high = value.astype(BF16)
    rest = value - high.astype(F32)
    mid = rest.astype(BF16)
    low = (rest - mid.astype(F32)).astype(BF16)
    return high, mid, low


def factor_kernel(table_ref, *refs, total_rows):
    right_ref, left_ref, state_ref = refs[-3:]
    width, size, _ = state_ref.shape
    half = size // 2
    each = width // 2
    scale = 1.0 / total_rows
    packed, diag = [], []
    for colour in range(2):
        total = added([ref[...] for ref in refs[colour * SIDE : (colour + 1) * SIDE]]) * scale
        tail = each * half
        exact = total[tail : tail + 8] + total[tail + 8 :]
        for m in range(each):
            packed.append(total[m * half : (m + 1) * half])
            diag.append(exact[m : m + 1])
    lane = iota2((half, size), 1)
    row2, lane2 = iota2((size, size), 0), iota2((size, size), 1)
    for m in range(width):
        p = packed[m]
        turned = jnp.concatenate([p, p], axis=0).T
        top = jnp.where(lane >= half, turned[:half], pltpu.roll(turned[half:], half, 1))
        upper = jnp.concatenate([top, p], axis=0)
        both = jnp.where(lane2 > row2, upper, upper.T)
        state_ref[m] = jnp.where(lane2 == row2, diag[m] + 0.1, both)

    deep = 16
    lanes, subs = iota2((deep, size), 1), iota2((deep, size), 0)
    for r0 in range(0, size, deep):
        panel = state_ref[:, r0 : r0 + deep, :]
        for k in range(deep):
            c = r0 + k
            col = panel[:, :, c : c + 1]
            pivot = panel[:, k : k + 1, c : c + 1]
            rk = lax.rsqrt(pivot)
            lead = jnp.where(lanes[:1] == c, rk, panel[:, k : k + 1, :] * rk)
            kept = jnp.where(lanes == c, 0.0, panel) - (col * rk) * lead
            panel = jnp.where(subs > k, kept, jnp.where(subs == k, lead, panel))
        rest = r0 + deep
        panel = jnp.where((lanes < rest) & (lanes > r0 + subs), 0.0, panel)
        state_ref[:, r0:rest, :] = panel
        if rest < size:
            h, m_, l = split3(panel)
            one = jnp.concatenate([h, h, h, m_, m_, l], axis=1)
            two = jnp.concatenate([h, m_, l, h, m_, h], axis=1)
            inside = (lane2[rest:] >= r0) & (lane2[rest:] < rest)
            for m in range(width):
                update = lax.dot_general(
                    one[m], two[m], (((0,), (0,)), ((), ())), preferred_element_type=F32
                )
                old = jnp.where(inside, 0.0, state_ref[m, rest:, :])
                state_ref[m, rest:, :] = old - update[rest:]

    for m in range(width):
        inverse = jnp.where(
            (lane2 <= row2) & (row2 < table_ref[2 * width + m]), state_ref[m], 0.0
        )
        high, low, _ = split3(inverse)
        left_ref[m] = jnp.concatenate([high, low, high], axis=1)
        high, low, _ = split3(inverse.T)
        right_ref[m] = jnp.concatenate([high, low], axis=1)


def inverse_factors(table, first, second, width, total_rows):
    size = first[0].shape[1]
    shapes = ((width, size, 2 * size), (width, size, 3 * size))
    vmem = pl.BlockSpec(memory_space=pltpu.VMEM)
    return pl.pallas_call(
        functools.partial(factor_kernel, total_rows=total_rows),
        out_shape=tuple(jax.ShapeDtypeStruct(s, BF16) for s in shapes),
        in_specs=[pl.BlockSpec(memory_space=pltpu.SMEM)] + [vmem] * (2 * SIDE),
        out_specs=(vmem, vmem),
        scratch_shapes=[pltpu.VMEM((width, size, size), F32)],
        name="factor",
    )(table, *first, *second)


def matvec_kernel(table_ref, v_ref, e_ref, w_ref, right_ref, left_ref, *rest, part, group):
    if part:
        _, o_ref, v_buf, wide_buf, y_buf, o_buf, sems = rest
    else:
        o_ref, wide_ref, v_buf, e_buf, wide_buf, y_buf, o_buf, sems = rest
    width, size, cols = v_buf.shape
    channels = w_ref.shape[0]
    span = pl.ds(part * cols, cols)
    copy = pltpu.make_async_copy
    v_in = [copy(v_ref.at[table_ref[i]], v_buf.at[i], sems.at[0, i]) for i in range(width)]
    e_to = wide_buf if part else e_buf
    e_in = [copy(e_ref.at[i], e_to.at[i], sems.at[1, i]) for i in range(width)]
    outs = [
        copy(o_buf.at[i], o_ref.at[table_ref[i], :, span], sems.at[2, i]) for i in range(width)
    ]
    for load in v_in + e_in:
        load.start()
    for i in range(width):
        v_in[i].wait()
        v = v_buf[i]
        y_buf[i] = jnp.dot(
            right_ref[i], jnp.concatenate([v, v], axis=0), preferred_element_type=F32
        )
    saves = []
    if not part:
        eye = (iota2((size, size), 0) == iota2((size, size), 1)).astype(BF16)
        first = table_ref[3 * width + 1] == 0

    def ready(i):
        e_in[i].wait()
        if part:
            return
        env = jnp.swapaxes(e_buf[i], 0, 1)
        for u in range(channels):
            block = jnp.where(first, eye, env[u]) if u == 0 else env[u]
            wide_buf[i, :, u * size : (u + 1) * size] = block
        saves.append(copy(wide_buf.at[i], wide_ref.at[i], sems.at[3, i]))
        saves[-1].start()

    def mixed(i):
        y = y_buf[i]
        total = None
        for w in range(0, channels, group):
            scaled = [
                (y * w_ref[u : u + 1, span]).astype(BF16) for u in range(w, w + group)
            ]
            piece = jnp.dot(
                wide_buf[i, :, w * size : (w + group) * size],
                jnp.concatenate(scaled, axis=0),
                preferred_element_type=F32,
            )
            total = piece if total is None else total + piece
        return total

    def finish(i, total):
        high = total.astype(BF16)
        low = (total - high.astype(F32)).astype(BF16)
        o_buf[i] = jnp.dot(
            left_ref[i], jnp.concatenate([high, high, low], axis=0), preferred_element_type=F32
        ).astype(BF16)
        outs[i].start()

    ready(0)
    before = None
    for i in range(width):
        if i + 1 < width:
            ready(i + 1)
        total = mixed(i)
        if i:
            finish(i - 1, before)
        before = total
    finish(width - 1, before)
    for out in outs + saves:
        out.wait()


def matvec(table, arrived, env, weights, right, left, part, filled, group=4):
    width, size, _ = right.shape
    channels, all_cols = weights.shape
    devices, _, cols = arrived.shape
    hbm = pl.BlockSpec(memory_space=pl.ANY)
    vmem = pl.BlockSpec(memory_space=pltpu.VMEM)
    out_shape = [jax.ShapeDtypeStruct((devices, size, all_cols), BF16)]
    wide = (width, size, channels * size)
    scratch = [pltpu.VMEM((width, size, cols), BF16)]
    if part == 0:
        out_shape.append(jax.ShapeDtypeStruct(wide, BF16))
        scratch.append(pltpu.VMEM(env.shape, BF16))
    scratch += [
        pltpu.VMEM(wide, BF16),
        pltpu.VMEM((width, size, cols), F32),
        pltpu.VMEM((width, size, cols), BF16),
        pltpu.SemaphoreType.DMA((4, width)),
    ]
    more = [] if part == 0 else [filled]
    return pl.pallas_call(
        functools.partial(matvec_kernel, part=part, group=group),
        out_shape=out_shape,
        in_specs=[pl.BlockSpec(memory_space=pltpu.SMEM), hbm, hbm, vmem, vmem, vmem]
        + [hbm] * len(more),
        out_specs=[hbm] * len(out_shape),
        scratch_shapes=scratch,
        input_output_aliases={6: 0} if more else {},
    )(table, arrived, env, weights, right, left, *more)


def gather_kernel(table_ref, x_ref, o_ref, buf_ref, sems):
    width = buf_ref.shape[0]
    loads = [
        pltpu.make_async_copy(x_ref.at[table_ref[width + j]], buf_ref.at[j], sems.at[0, j])
        for j in range(width)
    ]
    stores = [
        pltpu.make_async_copy(buf_ref.at[j], o_ref.at[j], sems.at[1, j]) for j in range(width)
    ]
    for load in loads:
        load.start()
    for load, store in zip(loads, stores):
        load.wait()
        store.start()
    for store in stores:
        store.wait()


def gathered(table, returned, width):
    _, size, cols = returned.shape
    hbm = pl.BlockSpec(memory_space=pl.ANY)
    shape = (width, size, cols)
    return pl.pallas_call(
        gather_kernel,
        out_shape=jax.ShapeDtypeStruct(shape, BF16),
        in_specs=[pl.BlockSpec(memory_space=pltpu.SMEM), hbm],
        out_specs=hbm,
        scratch_shapes=[pltpu.VMEM(shape, BF16), pltpu.SemaphoreType.DMA((2, width))],
        name="gather",
    )(table, returned)


def exchange(value):
    return lax.all_to_all(value, "sec", split_axis=0, concat_axis=0, tiled=True)


def on_device(
    wave_block, left_envs, next_vectors, site_weights, kept_counts, slots_before, slots_after
):
    width = left_envs.shape[1]
    total_rows = wave_block.shape[1] * lax.axis_size("sec")
    env = passed_along(left_envs[0], "seg", 1)
    sec, seg = [lax.axis_index(a).astype(jnp.int32).reshape(1) for a in ("sec", "seg")]
    table, packs, first, second = front(
        sec, seg, slots_before, slots_after, kept_counts, next_vectors[0], wave_block[0], PARTS
    )
    arrived = []
    for h in range(PARTS):
        arrived.append(exchange(packs[h]))
    first, second = turned_round(first, "x"), turned_round(second, "y")
    first, second = axis_sums(table, first, second, width)
    first, second = turned_round(first, "y"), turned_round(second, "x")
    right, left = inverse_factors(table, first, second, width, total_rows)
    result = None
    for h in range(PARTS):
        result, *wide = matvec(
            table, arrived[h], env, site_weights[0], right, left, h, result
        )
        env = wide[0] if wide else env
    returned = exchange(result)
    return gathered(table, returned, width)[None]


def solution(mesh):
    placed = (
        P("seg", "sec", None, None),
        P("seg", "sec", None, None, None),
        P("seg", "sec", None, None),
        P("seg", None, None),
        P(),
        P(),
        P(),
    )
    return jax.shard_map(
        on_device,
        mesh=mesh,
        in_specs=placed,
        out_specs=P("seg", "sec", None, None),
        check_vma=False,
    )
```
